32 devices in a mesh: pipe: 4 (over y, x), tensor: 8 (over z, core).
Axes of the slice: x: 2, y: 2, z: 4, core: 2. Of those that a mesh axis runs over, the one named last changes fastest.
Arguments:
- cotangent: bfloat16 [2, 128, 8192], P(None, 'tensor'), may hold values from -5 to 5
- inputs: bfloat16 [4, 2, 128, 8192], P('pipe', None, 'tensor'), may hold values from -24 to 24
- norm_gain: float32 [4, 8192], P('pipe'), may hold values from 0.1 to 1.9
- queries: bfloat16 [4, 2, 128, 4096], P('pipe', None, None, 'tensor'), may hold values from -4.6 to 4.6
- keys: bfloat16 [4, 2, 128, 4096], P('pipe', None, None, 'tensor'), may hold values from -4.6 to 4.6
- values: bfloat16 [4, 2, 128, 4096], P('pipe', None, None, 'tensor'), may hold values from -4 to 4
- qkv_weight: bfloat16 [4, 3, 8192, 4096], P('pipe', None, None, 'tensor'), may hold values from -0.0625 to 0.0625
- out_weight: bfloat16 [4, 4096, 8192], P('pipe', 'tensor'), may hold values from -0.09375 to 0.09375
- layout: int32 [2, 4, 4], replicated, may hold values from -1 to 3, as said below
Outputs:
- input_grads: bfloat16 [4, 2, 128, 8192], P('pipe', None, 'tensor')
The draws below stay inside these ranges and needn't reach their ends.
Inputs may be any that keep to these rules, and one draw needn't show every extreme that they name: `layout`: each entry is -1 (no block) or a key block not after its query block; the last entry of query block i is i and the one before it is i - 1 (or -1 for block 0); the first two entries are two blocks of the micro-batch that all later query blocks attend to.
All inputs are finite; a program needn't handle non-finite values.
Results may differ from the reference program's by a relative error of at most 0.02.
Values may be sent and summed in bfloat16 or wider, within the bound.
A program may use at most 128 MiB of HBM per device.

```python
import math
import jax
import jax.numpy as jnp
from jax import lax

D = 8192
HEADS = 32
HD = 128
SEQ = 128
MICRO = 2
BLOCK = 32
SECTIONS = 4
NB = 4
N_TENSOR = 8


def draw_queries(key, part):
    shape = (SECTIONS, MICRO, SEQ, HEADS * HD)
    base = jnp.clip(jax.random.normal(jax.random.fold_in(key, 1), shape, jnp.float32), -4.6, 4.6)
    return base.astype(jnp.bfloat16)


def draw_keys(key, part):
    shape = (SECTIONS, MICRO, SEQ, HEADS * HD)
    base = jnp.clip(jax.random.normal(jax.random.fold_in(key, 2), shape, jnp.float32), -4.6, 4.6)
    return base.astype(jnp.bfloat16)


def draw_inputs(key, part):
    shape = (SECTIONS, MICRO, SEQ, D)
    column_key, row_key, base_key = jax.random.split(key, 3)
    column_scale = jnp.exp(jax.random.uniform(column_key, (D,), jnp.float32, jnp.log(0.3), jnp.log(3.0)))
    row_scale = jnp.exp(jax.random.uniform(row_key, (SECTIONS, MICRO, SEQ, 1), jnp.float32, jnp.log(0.5), jnp.log(2.0)))
    base = jnp.clip(jax.random.normal(base_key, shape, jnp.float32), -4.0, 4.0)
    return (base * column_scale * row_scale).astype(jnp.bfloat16)


def draw_layout(key, part):
    first_key, second_key = jax.random.split(key)
    globals_one = jax.random.randint(first_key, (MICRO, 1), 0, NB)
    globals_two = jax.random.randint(second_key, (MICRO, 1), 0, NB)
    blocks = jnp.arange(NB, dtype=jnp.int32)[None, :]
    entry_one = jnp.where(globals_one <= blocks, globals_one, -1)
    entry_two = jnp.where(globals_two <= blocks, globals_two, -1)
    entry_prev = jnp.where(blocks >= 1, blocks - 1, -1)
    entry_self = jnp.broadcast_to(blocks, (MICRO, NB))
    return jnp.stack([entry_one, entry_two, jnp.broadcast_to(entry_prev, (MICRO, NB)), entry_self], -1).astype(jnp.int32)


def level_of(key, shape, cuts, low, high):
    def one(axis_at, shards_of):
        heights = jax.random.uniform(jax.random.fold_in(jax.random.fold_in(key, 6), axis_at), (shards_of,), jnp.float32, low / len(cuts), high / len(cuts))
        return jnp.repeat(jnp.exp(heights), shape[axis_at] // shards_of).reshape((-1,) + (1,) * (len(shape) - axis_at - 1))

    level = one(*cuts[0])
    for cut in cuts[1:]:
        level = level * one(*cut)
    return level


def noise(own_key, shape, width, most, cuts=(), kind=jnp.bfloat16):
    drawn = width * jax.random.normal(own_key, shape, jnp.float32)
    if cuts:
        drawn = drawn * level_of(own_key, shape, cuts, -0.22, 0.18)
    return jnp.clip(drawn, -most, most).astype(kind)


def setup_inputs(seed: int = 0) -> dict:
    arg_keys = jax.random.split(jax.random.key(seed), 10)
    cotangent = noise(arg_keys[0], (MICRO, SEQ, D), 1.0, 5.0, ((1, 8),))
    inputs = draw_inputs(jax.random.fold_in(arg_keys[9], 71), 0)
    norm_gain = jnp.clip(1.0 + 0.18 * jax.random.normal(arg_keys[2], (SECTIONS, D), jnp.float32), 0.1, 1.9)
    queries = draw_queries(jax.random.fold_in(arg_keys[9], 71), 0)
    keys = draw_keys(jax.random.fold_in(arg_keys[9], 71), 0)
    values = noise(arg_keys[5], (SECTIONS, MICRO, SEQ, HEADS * HD), 1.0, 4.0, ((0, 4), (3, 8)))
    qkv_weight = noise(arg_keys[6], (SECTIONS, 3, D, HEADS * HD), D ** -0.5, 0.0625, ((0, 4), (3, 8)))
    out_weight = noise(arg_keys[7], (SECTIONS, HEADS * HD, D), (HEADS * HD) ** -0.5, 0.09375, ((0, 4), (1, 8)))
    layout = draw_layout(jax.random.fold_in(arg_keys[9], 71), 0)
    return dict(cotangent=cotangent, inputs=inputs, norm_gain=norm_gain, queries=queries, keys=keys, values=values, qkv_weight=qkv_weight, out_weight=out_weight, layout=layout)


def block_mask(layout_rows):
    blocks = jnp.arange(NB, dtype=jnp.int32)
    listed = jnp.any(layout_rows[:, :, None] == blocks[None, None, :], axis=1)
    spread = jnp.broadcast_to(listed[:, None, :, None], (NB, BLOCK, NB, BLOCK)).reshape(SEQ, SEQ)
    places = jnp.arange(SEQ)
    return spread & (places[:, None] >= places[None, :])

def head_backward(query, key_rows, value_rows, out_grad, allowed):
    scale = 1.0 / math.sqrt(HD)
    scores = jnp.dot(query, key_rows.T, preferred_element_type=jnp.float32) * scale
    scores = jnp.where(allowed, scores, -1e+30)
    top = lax.optimization_barrier(jnp.max(scores, axis=1, keepdims=True))
    expo = jnp.exp(scores - top)
    probs = expo / lax.optimization_barrier(jnp.sum(expo, axis=1, keepdims=True))
    probs_half = probs.astype(jnp.bfloat16)
    attended = jnp.dot(probs_half, value_rows, preferred_element_type=jnp.float32)
    delta = lax.optimization_barrier(jnp.sum(out_grad.astype(jnp.float32) * attended, axis=1, keepdims=True))
    dprob = jnp.dot(out_grad, value_rows.T, preferred_element_type=jnp.float32)
    dscore = (probs * (dprob - delta)).astype(jnp.bfloat16)
    grad_query = (jnp.dot(dscore, key_rows, preferred_element_type=jnp.float32) * scale).astype(jnp.bfloat16)
    grad_key = (jnp.dot(dscore.T, query, preferred_element_type=jnp.float32) * scale).astype(jnp.bfloat16)
    grad_value = jnp.dot(probs_half.T, out_grad, preferred_element_type=jnp.float32).astype(jnp.bfloat16)
    return (grad_query, grad_key, grad_value)

def split_heads(array):
    return array.reshape(SEQ, HEADS, HD).transpose(1, 0, 2)

def join_heads(array):
    return array.transpose(1, 0, 2).reshape(SEQ, HEADS * HD)

def reference(cotangent, inputs, norm_gain, queries, keys, values, qkv_weight, out_weight, layout):
    groups = N_TENSOR
    columns = HEADS * HD // groups
    carried = [cotangent[micro] for micro in range(MICRO)]
    by_section = [None] * SECTIONS
    for section in range(SECTIONS - 1, -1, -1):
        produced = []
        for micro in range(MICRO):
            grad_rows = carried[micro]
            out_grad = jnp.dot(grad_rows, out_weight[section].T, preferred_element_type=jnp.float32).astype(jnp.bfloat16)
            allowed = block_mask(layout[micro])

            def per_head(items):
                return head_backward(items[0], items[1], items[2], items[3], allowed)
            grad_query, grad_key, grad_value = lax.map(per_head, (split_heads(queries[section, micro]), split_heads(keys[section, micro]), split_heads(values[section, micro]), split_heads(out_grad)))
            stacked = jnp.stack([join_heads(grad_query), join_heads(grad_key), join_heads(grad_value)], 0)
            weight = qkv_weight[section]

            def add_group(total, index):
                part = lax.dynamic_slice_in_dim(stacked, index * columns, columns, 2)
                weight_part = lax.dynamic_slice_in_dim(weight, index * columns, columns, 2)
                term = jnp.einsum('csn,cdn->sd', part.astype(jnp.float32), weight_part.astype(jnp.float32), precision=lax.Precision.HIGHEST)
                rounded = lax.optimization_barrier(term.astype(jnp.bfloat16))
                return (total + rounded.astype(jnp.float32), None)
            head_sum, _ = lax.scan(add_group, jnp.zeros((SEQ, D), jnp.float32), jnp.arange(groups, dtype=jnp.int32))
            x_rows = inputs[section, micro].astype(jnp.float32)
            factor = lax.rsqrt(lax.optimization_barrier(jnp.mean(x_rows * x_rows, axis=1, keepdims=True)) + 1e-05)
            normed = x_rows * factor
            scaled = head_sum * norm_gain[section][None, :]
            through = factor * (scaled - normed * lax.optimization_barrier(jnp.mean(scaled * normed, axis=1, keepdims=True)))
            produced.append((grad_rows.astype(jnp.float32) + through).astype(jnp.bfloat16))
        by_section[section] = jnp.stack(produced, 0)
        carried = produced
    return jnp.stack(by_section, 0)
```

```python
import functools
import math

import jax
import jax.numpy as jnp
from jax import lax
from jax.experimental import pallas as pl
from jax.experimental.pallas import tpu as pltpu
from jax.sharding import PartitionSpec as P

HD = 128
MESH = pl.DeviceIdType.MESH
NT = (((1,), (1,)), ((), ()))
TN = (((0,), (0,)), ((), ()))
NN = (((1,), (0,)), ((), ()))


def mm(a, b, dims):
    return lax.dot_general(a, b, dims, preferred_element_type=jnp.float32)


def body(
    sizes,
    layout, cot, xs, gain, qs, ks, vs, wqkv_hbm, wout_hbm,
    out,
    wqkv, wout, full, part, sibs, zsum, zgot, acc, grads, head,
    wout_sem, wqkv_sem, ag_s, ag_r, sg_s, sg_r, rb_s, rb_r, rz_s, rz_r, hop_s, hop_r,
):
    S, T, M, R, D, C, L, K, J, SUB = sizes
    Z = T // 2
    ck = D // K
    cj = D // J
    s = lax.axis_index("pipe")
    t = lax.axis_index("tensor")
    z = t // 2
    c = t % 2
    sib = z * 2 + (1 - c)
    scale = 1.0 / math.sqrt(HD)

    def kcols(k):
        return pl.ds(pl.multiple_of(k * ck, ck), ck)

    def jcols(j):
        return pl.ds(pl.multiple_of(j * cj, cj), cj)

    def peer(dz):
        return lax.rem(z + dz, Z) * 2 + c

    def origin(dz):
        return lax.rem(z + (Z - dz), Z) * 2 + c

    def wout_copy(k):
        return pltpu.make_async_copy(
            wout_hbm.at[0, :, kcols(k)], wout.at[:, kcols(k)], wout_sem.at[k]
        )

    def wqkv_copy(j):
        return pltpu.make_async_copy(
            wqkv_hbm.at[0, :, jcols(j), :], wqkv.at[:, jcols(j), :], wqkv_sem.at[j]
        )

    def remote(src, dst, ss, rs, device):
        return pltpu.make_async_remote_copy(
            src_ref=src, dst_ref=dst, send_sem=ss, recv_sem=rs,
            device_id=device, device_id_type=MESH,
        )

    def ag_out(m, k, dz):
        ref = full.at[m, t, :, kcols(k)]
        return remote(ref, ref, ag_s.at[m, k, dz - 1], ag_r.at[m, k, dz - 1], (s, peer(dz)))

    def ag_in(m, k, dz):
        ref = full.at[m, origin(dz), :, kcols(k)]
        return remote(ref, ref, ag_s.at[m, k, dz - 1], ag_r.at[m, k, dz - 1], (s, peer(dz)))

    def sg_out(m, k, dz):
        ref = full.at[m, origin(dz), :, kcols(k)]
        return remote(ref, ref, sg_s.at[m, k, dz], sg_r.at[m, k, dz], (s, sib))

    def sg_in(m, k, dz):
        ref = full.at[m, origin(dz) + 1 - 2 * c, :, kcols(k)]
        return remote(ref, ref, sg_s.at[m, k, dz], sg_r.at[m, k, dz], (s, sib))

    def rb(m, j):
        return remote(
            part.at[m, 1 - c, :, :, jcols(j)], sibs.at[m, :, :, jcols(j)],
            rb_s.at[m, j], rb_r.at[m, j], (s, sib),
        )

    def rz(m, j, dz):
        return remote(
            zsum.at[m, lax.rem(z + dz, Z), :, jcols(j)], zgot.at[m, dz - 1, :, jcols(j)],
            rz_s.at[m, j, dz - 1], rz_r.at[m, j, dz - 1], (s, peer(dz)),
        )

    def hop(m, k, section):
        return remote(
            out.at[m, :, kcols(k)], full.at[m, t, :, kcols(k)],
            hop_s.at[m, k], hop_r.at[m, k], (section, t),
        )

    def loop(n, fn):
        def step(i, carry):
            fn(i)
            return carry
        lax.fori_loop(0, n, step, 0)

    barrier = pltpu.get_barrier_semaphore()
    for dz in range(1, Z):
        pl.semaphore_signal(barrier, inc=1, device_id=(s, peer(dz)), device_id_type=MESH)
    pl.semaphore_signal(barrier, inc=1, device_id=(s, sib), device_id_type=MESH)

    @pl.when(s > 0)
    def _():
        pl.semaphore_signal(barrier, inc=1, device_id=(s - 1, t), device_id_type=MESH)

    @pl.when(s < S - 1)
    def _():
        pl.semaphore_signal(barrier, inc=1, device_id=(s + 1, t), device_id_type=MESH)

    loop(K, lambda k: wout_copy(k).start())
    loop(J, lambda j: wqkv_copy(j).start())
    ends = jnp.where(s == 0, 1, 0) + jnp.where(s == S - 1, 1, 0)
    pl.semaphore_wait(barrier, Z + 2 - ends)

    def micro(m):
        @pl.when(s == S - 1)
        def _():
            full[m, t] = cot[m]

        def spread(k):
            @pl.when(s < S - 1)
            def _():
                hop(m, k, s + 1).wait_recv()

            for dz in range(1, Z):
                ag_out(m, k, dz).start()
            sg_out(m, k, 0).start()

        loop(K, spread)
        acc[...] = jnp.zeros_like(acc)

        def gather(k):
            for dz in range(1, Z):
                ag_in(m, k, dz).wait_recv()
                sg_out(m, k, dz).start()

            @pl.when(m == 0)
            def _():
                wout_copy(k).wait()

            for dz in range(Z):
                sg_in(m, k, dz).wait_recv()
            rows = full[m, :, :, kcols(k)].reshape(L, ck)
            acc[...] += mm(rows, wout[:, kcols(k)], NT)

        loop(K, gather)

        nb = layout.shape[1]
        bl = L // nb
        kb = lax.broadcasted_iota(jnp.int32, (bl, L), 1) // bl
        strips = []
        for b in range(nb):
            strip = kb == layout[m, b, 0]
            for e in range(1, layout.shape[2]):
                strip = strip | (kb == layout[m, b, e])
            strips.append(jnp.where(strip, 1.0, 0.0))
        listed = jnp.concatenate(strips, axis=0)
        row = lax.broadcasted_iota(jnp.int32, (L, L), 0)
        col = lax.broadcasted_iota(jnp.int32, (L, L), 1)
        allowed = (listed > 0.5) & (col <= row)

        for h in range(C // HD):
            hc = slice(h * HD, (h + 1) * HD)
            query = qs[m, :, hc]
            key = ks[m, :, hc]
            value = vs[m, :, hc]
            go32 = acc[:, hc].astype(jnp.bfloat16)
            scores = jnp.where(allowed, mm(query, key, NT) * scale, -1e30)
            expo = jnp.exp(scores - jnp.max(scores, axis=1, keepdims=True))
            probs = expo / jnp.sum(expo, axis=1, keepdims=True)
            half = probs.astype(jnp.bfloat16)
            attended = mm(half, value, NN)
            delta = jnp.sum(attended * go32.astype(jnp.float32), axis=1, keepdims=True)
            dprob = mm(go32, value, NT)
            dscore = (probs * (dprob - delta)).astype(jnp.bfloat16)
            grads[0, :, hc] = (mm(dscore, key, NN) * scale).astype(jnp.bfloat16)
            grads[1, :, hc] = (mm(dscore, query, TN) * scale).astype(jnp.bfloat16)
            grads[2, :, hc] = mm(half, go32, TN).astype(jnp.bfloat16)

        def pair_sum(j):
            rb(m, j).wait_recv()

            def piece(i):
                cols = pl.ds(pl.multiple_of(j * cj + i * SUB, SUB), SUB)
                total = part[m, c, :, :, cols].astype(jnp.float32)
                total = total + sibs[m, :, :, cols].astype(jnp.float32)
                zsum[m, :, :, cols] = total.astype(jnp.bfloat16)

            loop(cj // SUB, piece)
            for dz in range(1, Z):
                rz(m, j, dz).start()

        def produce(j):
            @pl.when(m == 0)
            def _():
                wqkv_copy(j).wait()

            def piece(i):
                cols = pl.ds(pl.multiple_of(j * cj + i * SUB, SUB), SUB)
                value = mm(grads[0], wqkv[0, cols, :], NT)
                value = value + mm(grads[1], wqkv[1, cols, :], NT)
                value = value + mm(grads[2], wqkv[2, cols, :], NT)
                value = value.astype(jnp.bfloat16)
                for o in range(T):
                    part[m, o % 2, o // 2, :, cols] = value[o * R : (o + 1) * R]

            loop(cj // SUB, piece)
            rb(m, j).start()

            @pl.when(j > 0)
            def _():
                pair_sum(j - 1)

        loop(J, produce)
        pair_sum(J - 1)

        def settle(j, carry):
            for dz in range(1, Z):
                rz(m, j, dz).wait_recv()

            def piece(i, carry):
                squares, dots = carry
                cols = pl.ds(pl.multiple_of(j * cj + i * SUB, SUB), SUB)
                total = zsum[m, z, :, cols].astype(jnp.float32)
                for dz in range(1, Z):
                    total = total + zgot[m, dz - 1, :, cols].astype(jnp.float32)
                scaled = total * gain[:, cols]
                head[:, cols] = scaled
                x = xs[0, m, :, cols].astype(jnp.float32)
                squares = squares + jnp.sum(x * x, axis=1, keepdims=True)
                dots = dots + jnp.sum(x * scaled, axis=1, keepdims=True)
                return squares, dots

            return lax.fori_loop(0, cj // SUB, piece, carry)

        zero = jnp.zeros((R, 1), jnp.float32)
        squares, dots = lax.fori_loop(0, J, settle, (zero, zero))
        factor = lax.rsqrt(squares / D + 1e-05)
        inner = factor * factor * (dots / D)

        def finish(k):
            def piece(i):
                cols = pl.ds(pl.multiple_of(k * ck + i * SUB, SUB), SUB)
                x = xs[0, m, :, cols].astype(jnp.float32)
                through = factor * (head[:, cols] - x * inner)
                out[m, :, cols] = (
                    full[m, t, :, cols].astype(jnp.float32) + through
                ).astype(jnp.bfloat16)

            loop(ck // SUB, piece)

            @pl.when(s > 0)
            def _():
                hop(m, k, s - 1).start()

        loop(K, finish)

    loop(M, micro)

    def drain(m):
        def drain_k(k):
            for dz in range(1, Z):
                ag_out(m, k, dz).wait_send()
            for dz in range(Z):
                sg_out(m, k, dz).wait_send()

            @pl.when(s > 0)
            def _():
                hop(m, k, s - 1).wait_send()

        def drain_j(j):
            rb(m, j).wait_send()
            for dz in range(1, Z):
                rz(m, j, dz).wait_send()

        loop(K, drain_k)
        loop(J, drain_j)

    loop(M, drain)


def solution(mesh):
    S = mesh.shape["pipe"]
    T = mesh.shape["tensor"]

    def shards(cotangent, inputs, norm_gain, queries, keys, values, qkv_weight, out_weight, layout):
        M, R, D = cotangent.shape
        C = queries.shape[3]
        L = queries.shape[2]
        Z = T // 2
        K = 4
        J = 4
        SUB = 512
        sizes = (S, T, M, R, D, C, L, K, J, SUB)
        vmem = pl.BlockSpec(memory_space=pltpu.VMEM)
        hbm = pl.BlockSpec(memory_space=pl.ANY)
        bf = jnp.bfloat16
        dma = pltpu.SemaphoreType.DMA
        result = pl.pallas_call(
            functools.partial(body, sizes),
            out_shape=jax.ShapeDtypeStruct((M, R, D), bf),
            in_specs=[pl.BlockSpec(memory_space=pltpu.SMEM)] + [vmem] * 6 + [hbm] * 2,
            out_specs=vmem,
            scratch_shapes=[
                pltpu.VMEM((3, D, C), bf),
                pltpu.VMEM((C, D), bf),
                pltpu.VMEM((M, T, R, D), bf),
                pltpu.VMEM((M, 2, Z, R, D), bf),
                pltpu.VMEM((M, Z, R, D), bf),
                pltpu.VMEM((M, Z, R, D), bf),
                pltpu.VMEM((M, Z - 1, R, D), bf),
                pltpu.VMEM((L, C), jnp.float32),
                pltpu.VMEM((3, L, C), bf),
                pltpu.VMEM((R, D), jnp.float32),
                dma((K,)),
                dma((J,)),
                dma((M, K, Z - 1)),
                dma((M, K, Z - 1)),
                dma((M, K, Z)),
                dma((M, K, Z)),
                dma((M, J)),
                dma((M, J)),
                dma((M, J, Z - 1)),
                dma((M, J, Z - 1)),
                dma((M, K)),
                dma((M, K)),
            ],
            compiler_params=pltpu.CompilerParams(
                collective_id=0, has_side_effects=True, vmem_limit_bytes=60 * 1024 * 1024
            ),
        )(
            layout, cotangent, inputs, norm_gain, queries[0], keys[0], values[0],
            qkv_weight, out_weight,
        )
        return result[None]

    in_specs = (
        P(None, "tensor", None),
        P("pipe", None, "tensor", None),
        P("pipe", None),
        P("pipe", None, None, "tensor"),
        P("pipe", None, None, "tensor"),
        P("pipe", None, None, "tensor"),
        P("pipe", None, None, "tensor"),
        P("pipe", "tensor", None),
        P(),
    )
    out_specs = P("pipe", None, "tensor", None)
    return jax.shard_map(shards, mesh=mesh, in_specs=in_specs, out_specs=out_specs, check_vma=False)
```

```python
import functools
import math

import jax
import jax.numpy as jnp
from jax import lax
from jax.experimental import pallas as pl
from jax.experimental.pallas import tpu as pltpu
from jax.sharding import PartitionSpec as P

HD = 128
MESH = pl.DeviceIdType.MESH
NT = (((1,), (1,)), ((), ()))
TN = (((0,), (0,)), ((), ()))
NN = (((1,), (0,)), ((), ()))


def mm(a, b, dims):
    return lax.dot_general(a, b, dims, preferred_element_type=jnp.float32)


def body(
    sizes,
    layout, cot, xs, gain, qs, ks, vs, wqkv_hbm, wout_hbm,
    out,
    wqkv, wout, full, part, sibs, zsum, zgot, acc, grads, head, passed, probs_keep, att_keep,
    wout_sem, wqkv_sem, ag_s, ag_r, sg_s, sg_r, rb_s, rb_r, rz_s, rz_r, hop_s, hop_r,
    ra_s, ra_r, rf_s, rf_r,
):
    S, T, M, R, D, C, L, K, KB, J, SUB = sizes
    Z = T // 2
    ck = D // K
    cj = D // J
    s = lax.axis_index("pipe")
    t = lax.axis_index("tensor")
    z = t // 2
    c = t % 2
    sib = z * 2 + (1 - c)
    scale = 1.0 / math.sqrt(HD)

    def kcols(k):
        return pl.ds(pl.multiple_of(k * ck, ck), ck)

    def jcols(j):
        return pl.ds(pl.multiple_of(j * cj, cj), cj)

    def peer(dz):
        return lax.rem(z + dz, Z) * 2 + c

    def origin(dz):
        return lax.rem(z + (Z - dz), Z) * 2 + c

    def wout_copy(k):
        return pltpu.make_async_copy(
            wout_hbm.at[0, :, kcols(k)], wout.at[:, kcols(k)], wout_sem.at[k]
        )

    def wqkv_copy(j):
        return pltpu.make_async_copy(
            wqkv_hbm.at[0, :, jcols(j), :], wqkv.at[:, jcols(j), :], wqkv_sem.at[j]
        )

    def remote(src, dst, ss, rs, device):
        return pltpu.make_async_remote_copy(
            src_ref=src, dst_ref=dst, send_sem=ss, recv_sem=rs,
            device_id=device, device_id_type=MESH,
        )

    def ag_out(m, k, dz):
        ref = full.at[m, t, :, kcols(k)]
        return remote(ref, ref, ag_s.at[m, k, dz - 1], ag_r.at[m, k, dz - 1], (s, peer(dz)))

    def ag_in(m, k, dz):
        ref = full.at[m, origin(dz), :, kcols(k)]
        return remote(ref, ref, ag_s.at[m, k, dz - 1], ag_r.at[m, k, dz - 1], (s, peer(dz)))

    def sg_out(m, k, dz):
        ref = full.at[m, origin(dz), :, kcols(k)]
        return remote(ref, ref, sg_s.at[m, k, dz], sg_r.at[m, k, dz], (s, sib))

    def sg_in(m, k, dz):
        ref = full.at[m, origin(dz) + 1 - 2 * c, :, kcols(k)]
        return remote(ref, ref, sg_s.at[m, k, dz], sg_r.at[m, k, dz], (s, sib))

    def rb(m, j):
        return remote(
            part.at[m, 1 - c, :, :, jcols(j)], sibs.at[m, :, :, jcols(j)],
            rb_s.at[m, j], rb_r.at[m, j], (s, sib),
        )

    def rz(m, j, dz):
        return remote(
            zsum.at[m, lax.rem(z + dz, Z), :, jcols(j)], zgot.at[m, dz - 1, :, jcols(j)],
            rz_s.at[m, j, dz - 1], rz_r.at[m, j, dz - 1], (s, peer(dz)),
        )

    def hop(m, k, section):
        return remote(
            out.at[m, :, kcols(k)], full.at[m, t, :, kcols(k)],
            hop_s.at[m, k], hop_r.at[m, k], (section, t),
        )

    def acols(k):
        return pl.ds(pl.multiple_of((k - KB) * ck, ck), ck)

    def ra(m, k, dz):
        return remote(
            out.at[m, :, kcols(k)], passed.at[m, dz - 1, :, acols(k)],
            ra_s.at[m, k - KB, dz - 1], ra_r.at[m, k - KB, dz - 1], (s, peer(dz)),
        )

    def rf(m, k, dz, section):
        return remote(
            passed.at[m, dz - 1, :, acols(k)], full.at[m, origin(dz), :, kcols(k)],
            rf_s.at[m, k - KB, dz - 1], rf_r.at[m, k - KB, dz - 1], (section, t),
        )

    def loop(n, fn):
        def step(i, carry):
            fn(i)
            return carry
        lax.fori_loop(0, n, step, 0)

    barrier = pltpu.get_barrier_semaphore()
    for dz in range(1, Z):
        pl.semaphore_signal(barrier, inc=1, device_id=(s, peer(dz)), device_id_type=MESH)
    pl.semaphore_signal(barrier, inc=1, device_id=(s, sib), device_id_type=MESH)

    @pl.when(s > 0)
    def _():
        pl.semaphore_signal(barrier, inc=1, device_id=(s - 1, t), device_id_type=MESH)

    @pl.when(s < S - 1)
    def _():
        pl.semaphore_signal(barrier, inc=1, device_id=(s + 1, t), device_id_type=MESH)

    loop(K, lambda k: wout_copy(k).start())
    loop(J, lambda j: wqkv_copy(j).start())
    ends = jnp.where(s == 0, 1, 0) + jnp.where(s == S - 1, 1, 0)
    pl.semaphore_wait(barrier, Z + 2 - ends)

    def begin(m):
        @pl.when(s == S - 1)
        def _():
            full[m, t] = cot[m]

        def spread(k):
            @pl.when(s < S - 1)
            def _():
                hop(m, k, s + 1).wait_recv()

            @pl.when((s == S - 1) | (k < KB))
            def _():
                for dz in range(1, Z):
                    ag_out(m, k, dz).start()

            sg_out(m, k, 0).start()

        loop(K, spread)

    def micro(m):
        @pl.when((s < S - 1) | (m == 0))
        def _():
            begin(m)

        acc[...] = jnp.zeros_like(acc)
        nb = layout.shape[1]
        bl = L // nb
        kb = lax.broadcasted_iota(jnp.int32, (bl, L), 1) // bl
        strips = []
        for b in range(nb):
            strip = kb == layout[m, b, 0]
            for e in range(1, layout.shape[2]):
                strip = strip | (kb == layout[m, b, e])
            strips.append(jnp.where(strip, 1.0, 0.0))
        listed = jnp.concatenate(strips, axis=0)
        row = lax.broadcasted_iota(jnp.int32, (L, L), 0)
        col = lax.broadcasted_iota(jnp.int32, (L, L), 1)
        allowed = (listed > 0.5) & (col <= row)

        for h in range(C // HD):
            hc = slice(h * HD, (h + 1) * HD)
            scores = jnp.where(allowed, mm(qs[m, :, hc], ks[m, :, hc], NT) * scale, -1e30)
            expo = jnp.exp(scores - jnp.max(scores, axis=1, keepdims=True))
            probs = expo / jnp.sum(expo, axis=1, keepdims=True)
            probs_keep[h] = probs
            att_keep[:, hc] = mm(probs.astype(jnp.bfloat16), vs[m, :, hc], NN)

        def gather(k):
            for dz in range(1, Z):

                @pl.when((s == S - 1) | (k < KB))
                def _():
                    ag_in(m, k, dz).wait_recv()

                @pl.when((s < S - 1) & (k >= KB))
                def _():
                    rf(m, k, dz, s + 1).wait_recv()

                sg_out(m, k, dz).start()

            @pl.when(m == 0)
            def _():
                wout_copy(k).wait()

            for dz in range(Z):
                sg_in(m, k, dz).wait_recv()
            rows = full[m, :, :, kcols(k)].reshape(L, ck)
            acc[...] += mm(rows, wout[:, kcols(k)], NT)

        loop(K, gather)

        for h in range(C // HD):
            hc = slice(h * HD, (h + 1) * HD)
            query = qs[m, :, hc]
            key = ks[m, :, hc]
            value = vs[m, :, hc]
            go32 = acc[:, hc].astype(jnp.bfloat16)
            probs = probs_keep[h]
            half = probs.astype(jnp.bfloat16)
            delta = jnp.sum(att_keep[:, hc] * go32.astype(jnp.float32), axis=1, keepdims=True)
            dprob = mm(go32, value, NT)
            dscore = (probs * (dprob - delta)).astype(jnp.bfloat16)
            grads[0, :, hc] = (mm(dscore, key, NN) * scale).astype(jnp.bfloat16)
            grads[1, :, hc] = (mm(dscore, query, TN) * scale).astype(jnp.bfloat16)
            grads[2, :, hc] = mm(half, go32, TN).astype(jnp.bfloat16)

        def pair_sum(j):
            rb(m, j).wait_recv()

            def piece(i):
                cols = pl.ds(pl.multiple_of(j * cj + i * SUB, SUB), SUB)
                total = part[m, c, :, :, cols].astype(jnp.float32)
                total = total + sibs[m, :, :, cols].astype(jnp.float32)
                zsum[m, :, :, cols] = total.astype(jnp.bfloat16)

            loop(cj // SUB, piece)
            for dz in range(1, Z):
                rz(m, j, dz).start()

        def produce(j):
            @pl.when(m == 0)
            def _():
                wqkv_copy(j).wait()

            def piece(i):
                cols = pl.ds(pl.multiple_of(j * cj + i * SUB, SUB), SUB)
                value = mm(grads[0], wqkv[0, cols, :], NT)
                value = value + mm(grads[1], wqkv[1, cols, :], NT)
                value = value + mm(grads[2], wqkv[2, cols, :], NT)
                value = value.astype(jnp.bfloat16)
                for o in range(T):
                    part[m, o % 2, o // 2, :, cols] = value[o * R : (o + 1) * R]

            loop(cj // SUB, piece)
            rb(m, j).start()

            @pl.when(j > 0)
            def _():
                pair_sum(j - 1)

        loop(J, produce)
        pair_sum(J - 1)

        @pl.when((s == S - 1) & (m < M - 1))
        def _():
            begin(m + 1)

        def settle(j, carry):
            for dz in range(1, Z):
                rz(m, j, dz).wait_recv()

            def piece(i, carry):
                squares, dots = carry
                cols = pl.ds(pl.multiple_of(j * cj + i * SUB, SUB), SUB)
                total = zsum[m, z, :, cols].astype(jnp.float32)
                for dz in range(1, Z):
                    total = total + zgot[m, dz - 1, :, cols].astype(jnp.float32)
                scaled = total * gain[:, cols]
                head[:, cols] = scaled
                x = xs[0, m, :, cols].astype(jnp.float32)
                squares = squares + jnp.sum(x * x, axis=1, keepdims=True)
                dots = dots + jnp.sum(x * scaled, axis=1, keepdims=True)
                return squares, dots

            return lax.fori_loop(0, cj // SUB, piece, carry)

        zero = jnp.zeros((R, 1), jnp.float32)
        squares, dots = lax.fori_loop(0, J, settle, (zero, zero))
        factor = lax.rsqrt(squares / D + 1e-05)
        inner = factor * factor * (dots / D)

        def finish(k):
            def piece(i):
                cols = pl.ds(pl.multiple_of(k * ck + i * SUB, SUB), SUB)
                x = xs[0, m, :, cols].astype(jnp.float32)
                through = factor * (head[:, cols] - x * inner)
                out[m, :, cols] = (
                    full[m, t, :, cols].astype(jnp.float32) + through
                ).astype(jnp.bfloat16)

            loop(ck // SUB, piece)

            @pl.when(s > 0)
            def _():
                hop(m, k, s - 1).start()

                @pl.when(k >= KB)
                def _():
                    for dz in range(1, Z):
                        ra(m, k, dz).start()

        loop(K, finish)

        def pass_on(i):
            for dz in range(1, Z):
                ra(m, KB + i, dz).wait_recv()
                rf(m, KB + i, dz, s - 1).start()

        @pl.when(s > 0)
        def _():
            loop(K - KB, pass_on)

    loop(M, micro)

    def drain(m):
        def drain_k(k):
            @pl.when((s == S - 1) | (k < KB))
            def _():
                for dz in range(1, Z):
                    ag_out(m, k, dz).wait_send()

            for dz in range(Z):
                sg_out(m, k, dz).wait_send()

            @pl.when(s > 0)
            def _():
                hop(m, k, s - 1).wait_send()

                @pl.when(k >= KB)
                def _():
                    for dz in range(1, Z):
                        ra(m, k, dz).wait_send()
                        rf(m, k, dz, s - 1).wait_send()

        def drain_j(j):
            rb(m, j).wait_send()
            for dz in range(1, Z):
                rz(m, j, dz).wait_send()

        loop(K, drain_k)
        loop(J, drain_j)

    loop(M, drain)


def solution(mesh):
    S = mesh.shape["pipe"]
    T = mesh.shape["tensor"]

    def shards(cotangent, inputs, norm_gain, queries, keys, values, qkv_weight, out_weight, layout):
        M, R, D = cotangent.shape
        C = queries.shape[3]
        L = queries.shape[2]
        Z = T // 2
        K = 4
        KB = 2
        J = 8
        SUB = 512
        sizes = (S, T, M, R, D, C, L, K, KB, J, SUB)
        vmem = pl.BlockSpec(memory_space=pltpu.VMEM)
        hbm = pl.BlockSpec(memory_space=pl.ANY)
        bf = jnp.bfloat16
        dma = pltpu.SemaphoreType.DMA
        result = pl.pallas_call(
            functools.partial(body, sizes),
            out_shape=jax.ShapeDtypeStruct((M, R, D), bf),
            in_specs=[pl.BlockSpec(memory_space=pltpu.SMEM)] + [vmem] * 6 + [hbm] * 2,
            out_specs=vmem,
            scratch_shapes=[
                pltpu.VMEM((3, D, C), bf),
                pltpu.VMEM((C, D), bf),
                pltpu.VMEM((M, T, R, D), bf),
                pltpu.VMEM((M, 2, Z, R, D), bf),
                pltpu.VMEM((M, Z, R, D), bf),
                pltpu.VMEM((M, Z, R, D), bf),
                pltpu.VMEM((M, Z - 1, R, D), bf),
                pltpu.VMEM((L, C), jnp.float32),
                pltpu.VMEM((3, L, C), bf),
                pltpu.VMEM((R, D), jnp.float32),
                pltpu.VMEM((M, Z - 1, R, (K - KB) * (D // K)), bf),
                pltpu.VMEM((C // HD, L, L), jnp.float32),
                pltpu.VMEM((L, C), jnp.float32),
                dma((K,)),
                dma((J,)),
                dma((M, K, Z - 1)),
                dma((M, K, Z - 1)),
                dma((M, K, Z)),
                dma((M, K, Z)),
                dma((M, J)),
                dma((M, J)),
                dma((M, J, Z - 1)),
                dma((M, J, Z - 1)),
                dma((M, K)),
                dma((M, K)),
                dma((M, K - KB, Z - 1)),
                dma((M, K - KB, Z - 1)),
                dma((M, K - KB, Z - 1)),
                dma((M, K - KB, Z - 1)),
            ],
            compiler_params=pltpu.CompilerParams(
                collective_id=0, has_side_effects=True, vmem_limit_bytes=60 * 1024 * 1024
            ),
        )(
            layout, cotangent, inputs, norm_gain, queries[0], keys[0], values[0],
            qkv_weight, out_weight,
        )
        return result[None]

    in_specs = (
        P(None, "tensor", None),
        P("pipe", None, "tensor", None),
        P("pipe", None),
        P("pipe", None, None, "tensor"),
        P("pipe", None, None, "tensor"),
        P("pipe", None, None, "tensor"),
        P("pipe", None, None, "tensor"),
        P("pipe", "tensor", None),
        P(),
    )
    out_specs = P("pipe", None, "tensor", None)
    return jax.shard_map(shards, mesh=mesh, in_specs=in_specs, out_specs=out_specs, check_vma=False)
```

```python
import functools
import math

import jax
import jax.numpy as jnp
from jax import lax
from jax.experimental import pallas as pl
from jax.experimental.pallas import tpu as pltpu
from jax.sharding import PartitionSpec as P

HD = 128
MESH = pl.DeviceIdType.MESH
NT = (((1,), (1,)), ((), ()))
TN = (((0,), (0,)), ((), ()))
NN = (((1,), (0,)), ((), ()))


def mm(a, b, dims):
    return lax.dot_general(a, b, dims, preferred_element_type=jnp.float32)


def body(
    sizes,
    layout, cot, xs, gain, qs, ks, vs, wqkv_hbm, wout_hbm,
    out,
    wqkv, wout, full, part, sibs, zsum, zgot, acc, grads, head, passed, cpassed, probs_keep, att_keep,
    wout_sem, wqkv_sem, ag_s, ag_r, sg_s, sg_r, rb_s, rb_r, rz_s, rz_r, hop_s, hop_r,
    ra_s, ra_r, rf_s, rf_r, ca_s, ca_r, cf_s,
):
    S, T, M, R, D, C, L, K, KB, J, SUB = sizes
    Z = T // 2
    ck = D // K
    cj = D // J
    s = lax.axis_index("pipe")
    t = lax.axis_index("tensor")
    z = t // 2
    c = t % 2
    sib = z * 2 + (1 - c)
    scale = 1.0 / math.sqrt(HD)

    def kcols(k):
        return pl.ds(pl.multiple_of(k * ck, ck), ck)

    def jcols(j):
        return pl.ds(pl.multiple_of(j * cj, cj), cj)

    def peer(dz):
        return lax.rem(z + dz, Z) * 2 + c

    def origin(dz):
        return lax.rem(z + (Z - dz), Z) * 2 + c

    def wout_copy(k):
        return pltpu.make_async_copy(
            wout_hbm.at[0, :, kcols(k)], wout.at[:, kcols(k)], wout_sem.at[k]
        )

    def wqkv_copy(j):
        return pltpu.make_async_copy(
            wqkv_hbm.at[0, :, jcols(j), :], wqkv.at[:, jcols(j), :], wqkv_sem.at[j]
        )

    def remote(src, dst, ss, rs, device):
        return pltpu.make_async_remote_copy(
            src_ref=src, dst_ref=dst, send_sem=ss, recv_sem=rs,
            device_id=device, device_id_type=MESH,
        )

    def ag_out(m, k, dz):
        ref = full.at[m, t, :, kcols(k)]
        return remote(ref, ref, ag_s.at[m, k, dz - 1], ag_r.at[m, k, dz - 1], (s, peer(dz)))

    def ag_in(m, k, dz):
        ref = full.at[m, origin(dz), :, kcols(k)]
        return remote(ref, ref, ag_s.at[m, k, dz - 1], ag_r.at[m, k, dz - 1], (s, peer(dz)))

    def sg_out(m, k, dz):
        ref = full.at[m, origin(dz), :, kcols(k)]
        return remote(ref, ref, sg_s.at[m, k, dz], sg_r.at[m, k, dz], (s, sib))

    def sg_in(m, k, dz):
        ref = full.at[m, origin(dz) + 1 - 2 * c, :, kcols(k)]
        return remote(ref, ref, sg_s.at[m, k, dz], sg_r.at[m, k, dz], (s, sib))

    def rb(m, j):
        return remote(
            part.at[m, 1 - c, :, :, jcols(j)], sibs.at[m, :, :, jcols(j)],
            rb_s.at[m, j], rb_r.at[m, j], (s, sib),
        )

    def rz(m, j, dz):
        return remote(
            zsum.at[m, lax.rem(z + dz, Z), :, jcols(j)], zgot.at[m, dz - 1, :, jcols(j)],
            rz_s.at[m, j, dz - 1], rz_r.at[m, j, dz - 1], (s, peer(dz)),
        )

    def hop(m, k, section):
        return remote(
            out.at[m, :, kcols(k)], full.at[m, t, :, kcols(k)],
            hop_s.at[m, k], hop_r.at[m, k], (section, t),
        )

    def early(m, k):
        return (k >= KB) | (m == M - 1)

    def late(m, k):
        return (k < KB) & (m < M - 1)

    def ra(m, k, dz):
        return remote(
            out.at[m, :, kcols(k)], passed.at[m, dz - 1, :, kcols(k)],
            ra_s.at[m, k, dz - 1], ra_r.at[m, k, dz - 1], (s, peer(dz)),
        )

    def rf(m, k, dz, section):
        return remote(
            passed.at[m, dz - 1, :, kcols(k)], full.at[m, origin(dz), :, kcols(k)],
            rf_s.at[m, k, dz - 1], rf_r.at[m, k, dz - 1], (section, t),
        )

    def ca(m, k, dz):
        return remote(
            cot.at[m, :, kcols(k)], cpassed.at[m, dz - 1, :, kcols(k)],
            ca_s.at[m, k, dz - 1], ca_r.at[m, k, dz - 1], (s, peer(dz)),
        )

    def cf(m, k, dz):
        return remote(
            cpassed.at[m, dz - 1, :, kcols(k)], full.at[m, origin(dz), :, kcols(k)],
            cf_s.at[m, k, dz - 1], rf_r.at[m, k, dz - 1], (s + 1, t),
        )

    def loop(n, fn):
        def step(i, carry):
            fn(i)
            return carry
        lax.fori_loop(0, n, step, 0)

    barrier = pltpu.get_barrier_semaphore()
    for dz in range(1, Z):
        pl.semaphore_signal(barrier, inc=1, device_id=(s, peer(dz)), device_id_type=MESH)
    pl.semaphore_signal(barrier, inc=1, device_id=(s, sib), device_id_type=MESH)

    @pl.when(s > 0)
    def _():
        pl.semaphore_signal(barrier, inc=1, device_id=(s - 1, t), device_id_type=MESH)

    @pl.when(s < S - 1)
    def _():
        pl.semaphore_signal(barrier, inc=1, device_id=(s + 1, t), device_id_type=MESH)

    loop(K, lambda k: wout_copy(k).start())
    loop(J, lambda j: wqkv_copy(j).start())
    ends = jnp.where(s == 0, 1, 0) + jnp.where(s == S - 1, 1, 0)
    pl.semaphore_wait(barrier, Z + 2 - ends)

    source = jnp.where(s == S - 1, s - 1, s + 1)

    def each(fn):
        def outer(m):
            def inner(k):
                @pl.when(early(m, k))
                def _():
                    for dz in range(1, Z):
                        fn(m, k, dz)

            loop(K, inner)

        loop(M, outer)

    def relay(m, k, dz):
        ca(m, k, dz).wait_recv()
        cf(m, k, dz).start()

    @pl.when(s == S - 2)
    def _():
        each(lambda m, k, dz: ca(m, k, dz).start())
        each(relay)

    def begin(m):
        @pl.when(s == S - 1)
        def _():
            full[m, t] = cot[m]

        def spread(k):
            @pl.when(s < S - 1)
            def _():
                hop(m, k, s + 1).wait_recv()

            @pl.when(late(m, k))
            def _():
                for dz in range(1, Z):
                    ag_out(m, k, dz).start()

            sg_out(m, k, 0).start()

        loop(K, spread)

    def micro(m):
        begin(m)

        acc[...] = jnp.zeros_like(acc)
        nb = layout.shape[1]
        bl = L // nb
        kb = lax.broadcasted_iota(jnp.int32, (bl, L), 1) // bl
        strips = []
        for b in range(nb):
            strip = kb == layout[m, b, 0]
            for e in range(1, layout.shape[2]):
                strip = strip | (kb == layout[m, b, e])
            strips.append(jnp.where(strip, 1.0, 0.0))
        listed = jnp.concatenate(strips, axis=0)
        row = lax.broadcasted_iota(jnp.int32, (L, L), 0)
        col = lax.broadcasted_iota(jnp.int32, (L, L), 1)
        allowed = (listed > 0.5) & (col <= row)

        for h in range(C // HD):
            hc = slice(h * HD, (h + 1) * HD)
            scores = jnp.where(allowed, mm(qs[m, :, hc], ks[m, :, hc], NT) * scale, -1e30)
            expo = jnp.exp(scores - jnp.max(scores, axis=1, keepdims=True))
            probs = expo / jnp.sum(expo, axis=1, keepdims=True)
            probs_keep[h] = probs
            att_keep[:, hc] = mm(probs.astype(jnp.bfloat16), vs[m, :, hc], NN)

        def gather(k):
            for dz in range(1, Z):

                @pl.when(late(m, k))
                def _():
                    ag_in(m, k, dz).wait_recv()

                @pl.when(early(m, k))
                def _():
                    rf(m, k, dz, source).wait_recv()

                sg_out(m, k, dz).start()

            @pl.when(m == 0)
            def _():
                wout_copy(k).wait()

            for dz in range(Z):
                sg_in(m, k, dz).wait_recv()
            rows = full[m, :, :, kcols(k)].reshape(L, ck)
            acc[...] += mm(rows, wout[:, kcols(k)], NT)

        loop(K, gather)

        for h in range(C // HD):
            hc = slice(h * HD, (h + 1) * HD)
            query = qs[m, :, hc]
            key = ks[m, :, hc]
            value = vs[m, :, hc]
            go32 = acc[:, hc].astype(jnp.bfloat16)
            probs = probs_keep[h]
            half = probs.astype(jnp.bfloat16)
            delta = jnp.sum(att_keep[:, hc] * go32.astype(jnp.float32), axis=1, keepdims=True)
            dprob = mm(go32, value, NT)
            dscore = (probs * (dprob - delta)).astype(jnp.bfloat16)
            grads[0, :, hc] = (mm(dscore, key, NN) * scale).astype(jnp.bfloat16)
            grads[1, :, hc] = (mm(dscore, query, TN) * scale).astype(jnp.bfloat16)
            grads[2, :, hc] = mm(half, go32, TN).astype(jnp.bfloat16)

        def pair_sum(j):
            rb(m, j).wait_recv()

            def piece(i):
                cols = pl.ds(pl.multiple_of(j * cj + i * SUB, SUB), SUB)
                total = part[m, c, :, :, cols].astype(jnp.float32)
                total = total + sibs[m, :, :, cols].astype(jnp.float32)
                zsum[m, :, :, cols] = total.astype(jnp.bfloat16)

            loop(cj // SUB, piece)
            for dz in range(1, Z):
                rz(m, j, dz).start()

        def produce(j):
            @pl.when(m == 0)
            def _():
                wqkv_copy(j).wait()

            def piece(i):
                cols = pl.ds(pl.multiple_of(j * cj + i * SUB, SUB), SUB)
                value = mm(grads[0], wqkv[0, cols, :], NT)
                value = value + mm(grads[1], wqkv[1, cols, :], NT)
                value = value + mm(grads[2], wqkv[2, cols, :], NT)
                value = value.astype(jnp.bfloat16)
                for o in range(T):
                    part[m, o % 2, o // 2, :, cols] = value[o * R : (o + 1) * R]

            loop(cj // SUB, piece)
            rb(m, j).start()

            @pl.when(j > 0)
            def _():
                pair_sum(j - 1)

        loop(J, produce)
        pair_sum(J - 1)

        def settle(j, carry):
            for dz in range(1, Z):
                rz(m, j, dz).wait_recv()

            def piece(i, carry):
                squares, dots = carry
                cols = pl.ds(pl.multiple_of(j * cj + i * SUB, SUB), SUB)
                total = zsum[m, z, :, cols].astype(jnp.float32)
                for dz in range(1, Z):
                    total = total + zgot[m, dz - 1, :, cols].astype(jnp.float32)
                scaled = total * gain[:, cols]
                head[:, cols] = scaled
                x = xs[0, m, :, cols].astype(jnp.float32)
                squares = squares + jnp.sum(x * x, axis=1, keepdims=True)
                dots = dots + jnp.sum(x * scaled, axis=1, keepdims=True)
                return squares, dots

            return lax.fori_loop(0, cj // SUB, piece, carry)

        zero = jnp.zeros((R, 1), jnp.float32)
        squares, dots = lax.fori_loop(0, J, settle, (zero, zero))
        factor = lax.rsqrt(squares / D + 1e-05)
        inner = factor * factor * (dots / D)

        def finish(k):
            def piece(i):
                cols = pl.ds(pl.multiple_of(k * ck + i * SUB, SUB), SUB)
                x = xs[0, m, :, cols].astype(jnp.float32)
                through = factor * (head[:, cols] - x * inner)
                out[m, :, cols] = (
                    full[m, t, :, cols].astype(jnp.float32) + through
                ).astype(jnp.bfloat16)

            loop(ck // SUB, piece)

            @pl.when(s > 0)
            def _():
                hop(m, k, s - 1).start()

                @pl.when(early(m, k))
                def _():
                    for dz in range(1, Z):
                        ra(m, k, dz).start()

        loop(K, finish)

        def pass_on(k):
            @pl.when(early(m, k))
            def _():
                for dz in range(1, Z):
                    ra(m, k, dz).wait_recv()
                    rf(m, k, dz, s - 1).start()

        @pl.when(s > 0)
        def _():
            loop(K, pass_on)

    loop(M, micro)

    def drain(m):
        def drain_k(k):
            @pl.when(late(m, k))
            def _():
                for dz in range(1, Z):
                    ag_out(m, k, dz).wait_send()

            for dz in range(Z):
                sg_out(m, k, dz).wait_send()

            @pl.when(s > 0)
            def _():
                hop(m, k, s - 1).wait_send()

                @pl.when(early(m, k))
                def _():
                    for dz in range(1, Z):
                        ra(m, k, dz).wait_send()
                        rf(m, k, dz, s - 1).wait_send()

        def drain_j(j):
            rb(m, j).wait_send()
            for dz in range(1, Z):
                rz(m, j, dz).wait_send()

        loop(K, drain_k)
        loop(J, drain_j)

    loop(M, drain)

    def drain_relay(m, k, dz):
        ca(m, k, dz).wait_send()
        cf(m, k, dz).wait_send()

    @pl.when(s == S - 2)
    def _():
        each(drain_relay)


def solution(mesh):
    S = mesh.shape["pipe"]
    T = mesh.shape["tensor"]

    def shards(cotangent, inputs, norm_gain, queries, keys, values, qkv_weight, out_weight, layout):
        M, R, D = cotangent.shape
        C = queries.shape[3]
        L = queries.shape[2]
        Z = T // 2
        K = 4
        KB = 2
        J = 8
        SUB = 512
        sizes = (S, T, M, R, D, C, L, K, KB, J, SUB)
        vmem = pl.BlockSpec(memory_space=pltpu.VMEM)
        hbm = pl.BlockSpec(memory_space=pl.ANY)
        bf = jnp.bfloat16
        dma = pltpu.SemaphoreType.DMA
        result = pl.pallas_call(
            functools.partial(body, sizes),
            out_shape=jax.ShapeDtypeStruct((M, R, D), bf),
            in_specs=[pl.BlockSpec(memory_space=pltpu.SMEM)] + [vmem] * 6 + [hbm] * 2,
            out_specs=vmem,
            scratch_shapes=[
                pltpu.VMEM((3, D, C), bf),
                pltpu.VMEM((C, D), bf),
                pltpu.VMEM((M, T, R, D), bf),
                pltpu.VMEM((M, 2, Z, R, D), bf),
                pltpu.VMEM((M, Z, R, D), bf),
                pltpu.VMEM((M, Z, R, D), bf),
                pltpu.VMEM((M, Z - 1, R, D), bf),
                pltpu.VMEM((L, C), jnp.float32),
                pltpu.VMEM((3, L, C), bf),
                pltpu.VMEM((R, D), jnp.float32),
                pltpu.VMEM((M, Z - 1, R, D), bf),
                pltpu.VMEM((M, Z - 1, R, D), bf),
                pltpu.VMEM((C // HD, L, L), jnp.float32),
                pltpu.VMEM((L, C), jnp.float32),
                dma((K,)),
                dma((J,)),
                dma((M, K, Z - 1)),
                dma((M, K, Z - 1)),
                dma((M, K, Z)),
                dma((M, K, Z)),
                dma((M, J)),
                dma((M, J)),
                dma((M, J, Z - 1)),
                dma((M, J, Z - 1)),
                dma((M, K)),
                dma((M, K)),
                dma((M, K, Z - 1)),
                dma((M, K, Z - 1)),
                dma((M, K, Z - 1)),
                dma((M, K, Z - 1)),
                dma((M, K, Z - 1)),
                dma((M, K, Z - 1)),
                dma((M, K, Z - 1)),
            ],
            compiler_params=pltpu.CompilerParams(
                collective_id=0, has_side_effects=True, vmem_limit_bytes=60 * 1024 * 1024
            ),
        )(
            layout, cotangent, inputs, norm_gain, queries[0], keys[0], values[0],
            qkv_weight, out_weight,
        )
        return result[None]

    in_specs = (
        P(None, "tensor", None),
        P("pipe", None, "tensor", None),
        P("pipe", None),
        P("pipe", None, None, "tensor"),
        P("pipe", None, None, "tensor"),
        P("pipe", None, None, "tensor"),
        P("pipe", None, None, "tensor"),
        P("pipe", "tensor", None),
        P(),
    )
    out_specs = P("pipe", None, "tensor", None)
    return jax.shard_map(shards, mesh=mesh, in_specs=in_specs, out_specs=out_specs, check_vma=False)
```

```python
import functools
import math

import jax
import jax.numpy as jnp
from jax import lax
from jax.experimental import pallas as pl
from jax.experimental.pallas import tpu as pltpu
from jax.sharding import PartitionSpec as P

HD = 128
MESH = pl.DeviceIdType.MESH
NT = (((1,), (1,)), ((), ()))
TN = (((0,), (0,)), ((), ()))
NN = (((1,), (0,)), ((), ()))


def mm(a, b, dims):
    return lax.dot_general(a, b, dims, preferred_element_type=jnp.float32)


def body(
    sizes,
    layout, cot, xs, gain, qs, ks, vs, wqkv_hbm, wout_hbm,
    out,
    wqkv, wout, full, part, sibs, zsum, zgot, acc, grads, head, passed, cpassed, probs_keep, att_keep,
    wout_sem, wqkv_sem, ag_s, ag_r, sg_s, sg_r, rb_s, rb_r, rz_s, rz_r, hop_s, hop_r,
    ra_s, ra_r, rf_s, rf_r, ca_s, ca_r, cf_s,
):
    S, T, M, R, D, C, L, K, KB, J, SUB = sizes
    Z = T // 2
    ck = D // K
    cj = D // J
    s = lax.axis_index("pipe")
    t = lax.axis_index("tensor")
    z = t // 2
    c = t % 2
    sib = z * 2 + (1 - c)
    scale = 1.0 / math.sqrt(HD)

    def kcols(k):
        return pl.ds(pl.multiple_of(k * ck, ck), ck)

    def jcols(j):
        return pl.ds(pl.multiple_of(j * cj, cj), cj)

    def peer(dz):
        return lax.rem(z + dz, Z) * 2 + c

    def origin(dz):
        return lax.rem(z + (Z - dz), Z) * 2 + c

    def wout_copy(k):
        return pltpu.make_async_copy(
            wout_hbm.at[0, :, kcols(k)], wout.at[:, kcols(k)], wout_sem.at[k]
        )

    def wqkv_copy(j):
        return pltpu.make_async_copy(
            wqkv_hbm.at[0, :, jcols(j), :], wqkv.at[:, jcols(j), :], wqkv_sem.at[j]
        )

    def remote(src, dst, ss, rs, device):
        return pltpu.make_async_remote_copy(
            src_ref=src, dst_ref=dst, send_sem=ss, recv_sem=rs,
            device_id=device, device_id_type=MESH,
        )

    def ag_out(m, k, dz):
        ref = full.at[m, t, :, kcols(k)]
        return remote(ref, ref, ag_s.at[m, k, dz - 1], ag_r.at[m, k, dz - 1], (s, peer(dz)))

    def ag_in(m, k, dz):
        ref = full.at[m, origin(dz), :, kcols(k)]
        return remote(ref, ref, ag_s.at[m, k, dz - 1], ag_r.at[m, k, dz - 1], (s, peer(dz)))

    def sg_out(m, k, dz):
        ref = full.at[m, origin(dz), :, kcols(k)]
        return remote(ref, ref, sg_s.at[m, k, dz], sg_r.at[m, k, dz], (s, sib))

    def sg_in(m, k, dz):
        ref = full.at[m, origin(dz) + 1 - 2 * c, :, kcols(k)]
        return remote(ref, ref, sg_s.at[m, k, dz], sg_r.at[m, k, dz], (s, sib))

    def rb(m, j):
        return remote(
            part.at[m, 1 - c, :, :, jcols(j)], sibs.at[m, :, :, jcols(j)],
            rb_s.at[m, j], rb_r.at[m, j], (s, sib),
        )

    def rz(m, j, dz):
        return remote(
            zsum.at[m, lax.rem(z + dz, Z), :, jcols(j)], zgot.at[m, dz - 1, :, jcols(j)],
            rz_s.at[m, j, dz - 1], rz_r.at[m, j, dz - 1], (s, peer(dz)),
        )

    def hop(m, k, section):
        return remote(
            out.at[m, :, kcols(k)], full.at[m, t, :, kcols(k)],
            hop_s.at[m, k], hop_r.at[m, k], (section, t),
        )

    def early(m, k):
        return k >= KB

    def late(m, k):
        return k < KB

    def ra(m, k, dz):
        return remote(
            out.at[m, :, kcols(k)], passed.at[m, dz - 1, :, kcols(k)],
            ra_s.at[m, k, dz - 1], ra_r.at[m, k, dz - 1], (s, peer(dz)),
        )

    def rf(m, k, dz, section):
        return remote(
            passed.at[m, dz - 1, :, kcols(k)], full.at[m, origin(dz), :, kcols(k)],
            rf_s.at[m, k, dz - 1], rf_r.at[m, k, dz - 1], (section, t),
        )

    def ca(m, k, dz):
        return remote(
            cot.at[m, :, kcols(k)], cpassed.at[m, dz - 1, :, kcols(k)],
            ca_s.at[m, k, dz - 1], ca_r.at[m, k, dz - 1], (s, peer(dz)),
        )

    def cf(m, k, dz):
        return remote(
            cpassed.at[m, dz - 1, :, kcols(k)], full.at[m, origin(dz), :, kcols(k)],
            cf_s.at[m, k, dz - 1], rf_r.at[m, k, dz - 1], (s + 1, t),
        )

    def loop(n, fn):
        def step(i, carry):
            fn(i)
            return carry
        lax.fori_loop(0, n, step, 0)

    barrier = pltpu.get_barrier_semaphore()
    for dz in range(1, Z):
        pl.semaphore_signal(barrier, inc=1, device_id=(s, peer(dz)), device_id_type=MESH)
    pl.semaphore_signal(barrier, inc=1, device_id=(s, sib), device_id_type=MESH)

    @pl.when(s > 0)
    def _():
        pl.semaphore_signal(barrier, inc=1, device_id=(s - 1, t), device_id_type=MESH)

    @pl.when(s < S - 1)
    def _():
        pl.semaphore_signal(barrier, inc=1, device_id=(s + 1, t), device_id_type=MESH)

    loop(K, lambda k: wout_copy(k).start())
    loop(J, lambda j: wqkv_copy(j).start())
    ends = jnp.where(s == 0, 1, 0) + jnp.where(s == S - 1, 1, 0)
    pl.semaphore_wait(barrier, Z + 2 - ends)

    source = jnp.where(s == S - 1, s - 1, s + 1)

    def each(fn):
        def outer(m):
            def inner(k):
                @pl.when(early(m, k))
                def _():
                    for dz in range(1, Z):
                        fn(m, k, dz)

            loop(K, inner)

        loop(M, outer)

    def relay(m, k, dz):
        ca(m, k, dz).wait_recv()
        cf(m, k, dz).start()

    @pl.when(s == S - 2)
    def _():
        each(lambda m, k, dz: ca(m, k, dz).start())
        each(relay)

    def begin(m):
        @pl.when(s == S - 1)
        def _():
            full[m, t] = cot[m]

        def spread(k):
            @pl.when(s < S - 1)
            def _():
                hop(m, k, s + 1).wait_recv()

            @pl.when(late(m, k))
            def _():
                for dz in range(1, Z):
                    ag_out(m, k, dz).start()

            sg_out(m, k, 0).start()

        loop(K, spread)

    def micro(m):
        begin(m)

        acc[...] = jnp.zeros_like(acc)
        nb = layout.shape[1]
        bl = L // nb
        kb = lax.broadcasted_iota(jnp.int32, (bl, L), 1) // bl
        strips = []
        for b in range(nb):
            strip = kb == layout[m, b, 0]
            for e in range(1, layout.shape[2]):
                strip = strip | (kb == layout[m, b, e])
            strips.append(jnp.where(strip, 1.0, 0.0))
        listed = jnp.concatenate(strips, axis=0)
        row = lax.broadcasted_iota(jnp.int32, (L, L), 0)
        col = lax.broadcasted_iota(jnp.int32, (L, L), 1)
        allowed = (listed > 0.5) & (col <= row)

        for h in range(C // HD):
            hc = slice(h * HD, (h + 1) * HD)
            scores = jnp.where(allowed, mm(qs[m, :, hc], ks[m, :, hc], NT) * scale, -1e30)
            expo = jnp.exp(scores - jnp.max(scores, axis=1, keepdims=True))
            probs = expo / jnp.sum(expo, axis=1, keepdims=True)
            probs_keep[h] = probs
            att_keep[:, hc] = mm(probs.astype(jnp.bfloat16), vs[m, :, hc], NN)

        def gather(k):
            for dz in range(1, Z):

                @pl.when(late(m, k))
                def _():
                    ag_in(m, k, dz).wait_recv()

                @pl.when(early(m, k))
                def _():
                    rf(m, k, dz, source).wait_recv()

                sg_out(m, k, dz).start()

            @pl.when(m == 0)
            def _():
                wout_copy(k).wait()

            for dz in range(Z):
                sg_in(m, k, dz).wait_recv()
            rows = full[m, :, :, kcols(k)].reshape(L, ck)
            acc[...] += mm(rows, wout[:, kcols(k)], NT)

        loop(K, gather)

        for h in range(C // HD):
            hc = slice(h * HD, (h + 1) * HD)
            query = qs[m, :, hc]
            key = ks[m, :, hc]
            value = vs[m, :, hc]
            go32 = acc[:, hc].astype(jnp.bfloat16)
            probs = probs_keep[h]
            half = probs.astype(jnp.bfloat16)
            delta = jnp.sum(att_keep[:, hc] * go32.astype(jnp.float32), axis=1, keepdims=True)
            dprob = mm(go32, value, NT)
            dscore = (probs * (dprob - delta)).astype(jnp.bfloat16)
            grads[0, :, hc] = (mm(dscore, key, NN) * scale).astype(jnp.bfloat16)
            grads[1, :, hc] = (mm(dscore, query, TN) * scale).astype(jnp.bfloat16)
            grads[2, :, hc] = mm(half, go32, TN).astype(jnp.bfloat16)

        def pair_sum(j):
            rb(m, j).wait_recv()

            def piece(i):
                cols = pl.ds(pl.multiple_of(j * cj + i * SUB, SUB), SUB)
                total = part[m, c, :, :, cols].astype(jnp.float32)
                total = total + sibs[m, :, :, cols].astype(jnp.float32)
                zsum[m, :, :, cols] = total.astype(jnp.bfloat16)

            loop(cj // SUB, piece)
            for dz in range(1, Z):
                rz(m, j, dz).start()

        def produce(j):
            @pl.when(m == 0)
            def _():
                wqkv_copy(j).wait()

            def piece(i):
                cols = pl.ds(pl.multiple_of(j * cj + i * SUB, SUB), SUB)
                value = mm(grads[0], wqkv[0, cols, :], NT)
                value = value + mm(grads[1], wqkv[1, cols, :], NT)
                value = value + mm(grads[2], wqkv[2, cols, :], NT)
                value = value.astype(jnp.bfloat16)
                for o in range(T):
                    part[m, o % 2, o // 2, :, cols] = value[o * R : (o + 1) * R]

            loop(cj // SUB, piece)
            rb(m, j).start()

            @pl.when(j > 0)
            def _():
                pair_sum(j - 1)

        loop(J, produce)
        pair_sum(J - 1)

        def settle(j, carry):
            for dz in range(1, Z):
                rz(m, j, dz).wait_recv()

            def piece(i, carry):
                squares, dots = carry
                cols = pl.ds(pl.multiple_of(j * cj + i * SUB, SUB), SUB)
                total = zsum[m, z, :, cols].astype(jnp.float32)
                for dz in range(1, Z):
                    total = total + zgot[m, dz - 1, :, cols].astype(jnp.float32)
                scaled = total * gain[:, cols]
                head[:, cols] = scaled
                x = xs[0, m, :, cols].astype(jnp.float32)
                squares = squares + jnp.sum(x * x, axis=1, keepdims=True)
                dots = dots + jnp.sum(x * scaled, axis=1, keepdims=True)
                return squares, dots

            return lax.fori_loop(0, cj // SUB, piece, carry)

        zero = jnp.zeros((R, 1), jnp.float32)
        squares, dots = lax.fori_loop(0, J, settle, (zero, zero))
        factor = lax.rsqrt(squares / D + 1e-05)
        inner = factor * factor * (dots / D)

        def finish(k):
            def piece(i):
                cols = pl.ds(pl.multiple_of(k * ck + i * SUB, SUB), SUB)
                x = xs[0, m, :, cols].astype(jnp.float32)
                through = factor * (head[:, cols] - x * inner)
                out[m, :, cols] = (
                    full[m, t, :, cols].astype(jnp.float32) + through
                ).astype(jnp.bfloat16)

            loop(ck // SUB, piece)

            @pl.when(s > 0)
            def _():
                hop(m, k, s - 1).start()

                @pl.when(early(m, k))
                def _():
                    for dz in range(1, Z):
                        ra(m, k, dz).start()

        loop(K, finish)

        def pass_on(k):
            @pl.when(early(m, k))
            def _():
                for dz in range(1, Z):
                    ra(m, k, dz).wait_recv()
                    rf(m, k, dz, s - 1).start()

        @pl.when(s > 0)
        def _():
            loop(K, pass_on)

    loop(M, micro)

    def drain(m):
        def drain_k(k):
            @pl.when(late(m, k))
            def _():
                for dz in range(1, Z):
                    ag_out(m, k, dz).wait_send()

            for dz in range(Z):
                sg_out(m, k, dz).wait_send()

            @pl.when(s > 0)
            def _():
                hop(m, k, s - 1).wait_send()

                @pl.when(early(m, k))
                def _():
                    for dz in range(1, Z):
                        ra(m, k, dz).wait_send()
                        rf(m, k, dz, s - 1).wait_send()

        def drain_j(j):
            rb(m, j).wait_send()
            for dz in range(1, Z):
                rz(m, j, dz).wait_send()

        loop(K, drain_k)
        loop(J, drain_j)

    loop(M, drain)

    def drain_relay(m, k, dz):
        ca(m, k, dz).wait_send()
        cf(m, k, dz).wait_send()

    @pl.when(s == S - 2)
    def _():
        each(drain_relay)


def solution(mesh):
    S = mesh.shape["pipe"]
    T = mesh.shape["tensor"]

    def shards(cotangent, inputs, norm_gain, queries, keys, values, qkv_weight, out_weight, layout):
        M, R, D = cotangent.shape
        C = queries.shape[3]
        L = queries.shape[2]
        Z = T // 2
        K = 8
        KB = 4
        J = 8
        SUB = 512
        sizes = (S, T, M, R, D, C, L, K, KB, J, SUB)
        vmem = pl.BlockSpec(memory_space=pltpu.VMEM)
        hbm = pl.BlockSpec(memory_space=pl.ANY)
        bf = jnp.bfloat16
        dma = pltpu.SemaphoreType.DMA
        result = pl.pallas_call(
            functools.partial(body, sizes),
            out_shape=jax.ShapeDtypeStruct((M, R, D), bf),
            in_specs=[pl.BlockSpec(memory_space=pltpu.SMEM)] + [vmem] * 6 + [hbm] * 2,
            out_specs=vmem,
            scratch_shapes=[
                pltpu.VMEM((3, D, C), bf),
                pltpu.VMEM((C, D), bf),
                pltpu.VMEM((M, T, R, D), bf),
                pltpu.VMEM((M, 2, Z, R, D), bf),
                pltpu.VMEM((M, Z, R, D), bf),
                pltpu.VMEM((M, Z, R, D), bf),
                pltpu.VMEM((M, Z - 1, R, D), bf),
                pltpu.VMEM((L, C), jnp.float32),
                pltpu.VMEM((3, L, C), bf),
                pltpu.VMEM((R, D), jnp.float32),
                pltpu.VMEM((M, Z - 1, R, D), bf),
                pltpu.VMEM((M, Z - 1, R, D), bf),
                pltpu.VMEM((C // HD, L, L), jnp.float32),
                pltpu.VMEM((L, C), jnp.float32),
                dma((K,)),
                dma((J,)),
                dma((M, K, Z - 1)),
                dma((M, K, Z - 1)),
                dma((M, K, Z)),
                dma((M, K, Z)),
                dma((M, J)),
                dma((M, J)),
                dma((M, J, Z - 1)),
                dma((M, J, Z - 1)),
                dma((M, K)),
                dma((M, K)),
                dma((M, K, Z - 1)),
                dma((M, K, Z - 1)),
                dma((M, K, Z - 1)),
                dma((M, K, Z - 1)),
                dma((M, K, Z - 1)),
                dma((M, K, Z - 1)),
                dma((M, K, Z - 1)),
            ],
            compiler_params=pltpu.CompilerParams(
                collective_id=0, has_side_effects=True, vmem_limit_bytes=60 * 1024 * 1024
            ),
        )(
            layout, cotangent, inputs, norm_gain, queries[0], keys[0], values[0],
            qkv_weight, out_weight,
        )
        return result[None]

    in_specs = (
        P(None, "tensor", None),
        P("pipe", None, "tensor", None),
        P("pipe", None),
        P("pipe", None, None, "tensor"),
        P("pipe", None, None, "tensor"),
        P("pipe", None, None, "tensor"),
        P("pipe", None, None, "tensor"),
        P("pipe", "tensor", None),
        P(),
    )
    out_specs = P("pipe", None, "tensor", None)
    return jax.shard_map(shards, mesh=mesh, in_specs=in_specs, out_specs=out_specs, check_vma=False)
```
